512 devices in a mesh: tm: 32 (over z, core), basis: 16 (over x, y).
Axes of the slice: x: 4, y: 4, z: 16, core: 2. Of those that a mesh axis runs over, the one named last changes fastest.
Arguments:
- propagators: bfloat16 [32, 96, 7, 128, 128], P('tm', 'basis'), may hold values from -0.1875 to 0.1875
- probes: bfloat16 [32, 96, 16, 128], P('tm', 'basis'), may hold values from -6 to 6
- block_cols: int32 [96, 7], P('basis'), may hold values from 0 to 95, as said below
Outputs:
- gradient: bfloat16 [32, 96, 7, 128, 128], P('tm', 'basis')
The draws below stay inside these ranges and needn't reach their ends.
Inputs may be any that keep to these rules, and one draw needn't show every extreme that they name: `block_cols`: within the block rows of one device, at most 2 entries name block rows of any one other device (the device of block row j is j // 6); in every draw there is one device whose block rows are named exactly 2 times from the block rows of every other device; other pairs of devices may have 0, 1 or 2 such entries.
All inputs are finite; a program needn't handle non-finite values.
Results may differ from the reference program's by a relative error of at most 0.04.
Values may be sent and summed in bfloat16 or wider, within the bound.
No kernel may reach another device: no remote copies, remote signals or barrier semaphores. Data moves between devices by JAX's collectives and lax.ppermute only.
A program may use at most 64 MiB of HBM per device.

```python
import math
import jax
import jax.numpy as jnp
from jax import lax

BLK = 128
NBR = 7
CAP = 2
R_DEV = 6
PROBES = 16
SLICES = 32
NBLK = 96


def draw_block_cols(key, part):
    devices = NBLK // R_DEV
    entries = NBR * R_DEV
    key_hot, key_count, key_offset, key_order = jax.random.split(key, 4)
    hot_device = jax.random.randint(key_hot, (), 0, devices)
    counts = jax.random.randint(key_count, (devices, devices), 0, CAP + 1)
    device_ids = jnp.arange(devices, dtype=jnp.int32)
    counts = jnp.where(device_ids[None, :] == hot_device, CAP, counts)
    counts = jnp.where(device_ids[:, None] == device_ids[None, :], 0, counts)
    peer_order = (device_ids[:, None] + jnp.arange(1, devices, dtype=jnp.int32)[None, :]) % devices
    peer_counts = jnp.take_along_axis(counts, peer_order, 1)
    bounds = jnp.cumsum(peer_counts, 1)
    positions = jnp.arange(entries, dtype=jnp.int32)
    segment = jnp.sum((positions[None, :, None] >= bounds[:, None, :]).astype(jnp.int32), -1)
    picked = jnp.take_along_axis(peer_order, jnp.clip(segment, 0, devices - 2), 1)
    owners = jnp.where(segment < devices - 1, picked, device_ids[:, None])
    offsets = jax.random.randint(key_offset, (devices, entries), 0, R_DEV)
    columns = owners * R_DEV + offsets
    orders = jax.vmap(lambda single: jax.random.permutation(single, entries))(jax.random.split(key_order, devices))
    shuffled = jnp.take_along_axis(columns, orders, 1)
    return shuffled.reshape(NBLK, NBR).astype(jnp.int32)


def steps_of(key, extent, pieces, smallest, top_value):
    level = 1.0
    for dim, parts in pieces:
        draws = jax.random.uniform(jax.random.fold_in(jax.random.fold_in(key, 6), dim), (parts,), jnp.float32, smallest / len(pieces), top_value / len(pieces))
        level = level * jnp.repeat(jnp.exp(draws), extent[dim] // parts).reshape((-1,) + (1,) * (len(extent) - 1 - dim))
    return level


def bell_draw(key, shape, spread, most, pieces=(), kind=jnp.bfloat16):
    level = steps_of(key, shape, pieces, -0.22, 0.18) if pieces else 1.0
    drawn = jax.random.normal(key, shape, jnp.float32) * spread * level
    return jnp.minimum(jnp.maximum(drawn, -most), most).astype(kind)


def setup_inputs(seed: int = 0) -> dict:
    key_of = jax.random.split(jax.random.key(seed), 4)
    return {
        "propagators": bell_draw(key_of[0], (SLICES, NBLK, NBR, BLK, BLK), (NBR * BLK) ** -0.5, 0.1875, ((0, 32), (1, 16))),
        "probes": bell_draw(key_of[1], (SLICES, NBLK, PROBES, BLK), 1.0, 6.0, ((0, 32), (1, 16))),
        "block_cols": draw_block_cols(jax.random.fold_in(key_of[3], 71), 0),
    }


def forward_image(slice_blocks, visitor, block_cols):
    entry_blocks = visitor[block_cols].astype(jnp.float32)
    images = jnp.einsum('nkpb,nkab->npa', entry_blocks, slice_blocks.astype(jnp.float32))
    return images.astype(jnp.bfloat16)

def adjoint_image(slice_blocks, adjoint, block_cols, remote):
    contrib = jnp.einsum('npa,nkab->nkpb', adjoint.astype(jnp.float32), slice_blocks.astype(jnp.float32))
    rounded = lax.optimization_barrier(contrib.astype(jnp.bfloat16)).astype(jnp.float32)
    contrib = jnp.where(remote[:, :, None, None], rounded, contrib)
    summed = jax.ops.segment_sum(contrib.reshape(NBLK * NBR, PROBES, BLK), block_cols.reshape(-1), num_segments=NBLK)
    return summed.astype(jnp.bfloat16)

def reference(propagators, probes, block_cols):
    row_owner = (jnp.arange(NBLK, dtype=jnp.int32) // R_DEV)[:, None]
    remote = block_cols // R_DEV != row_owner

    def forward_one(couple):
        return forward_image(couple[0], couple[1], block_cols)

    def adjoint_one(couple):
        return adjoint_image(couple[0], couple[1], block_cols, remote)

    def forward_turn(visitors, unused):
        images = lax.map(forward_one, (propagators, visitors))
        return (jnp.roll(images, 1, 0), visitors)

    def adjoint_turn(adjoints, unused):
        images = lax.map(adjoint_one, (propagators, adjoints))
        return (jnp.roll(images, -1, 0), adjoints)
    _, forward_store = lax.scan(forward_turn, probes, None, length=SLICES)
    _, adjoint_store = lax.scan(adjoint_turn, jnp.roll(probes, -1, 0), None, length=SLICES)
    reversed_store = adjoint_store[::-1]
    grad_scale = 1.0 / math.sqrt(SLICES * PROBES)

    def slice_gradient(slice_index):
        visits = forward_store[:, slice_index]
        adjoints = reversed_store[:, slice_index].astype(jnp.float32)
        entry_blocks = visits[:, block_cols].astype(jnp.float32)
        summed = jnp.einsum('hnpa,hnkpb->nkab', adjoints, entry_blocks)
        return (summed * grad_scale).astype(jnp.bfloat16)
    return lax.map(slice_gradient, jnp.arange(SLICES, dtype=jnp.int32))
```

```python
import functools
import math

import jax
import jax.numpy as jnp
from jax import lax
from jax.experimental import pallas as pl
from jax.experimental.pallas import tpu as pltpu
from jax.sharding import PartitionSpec as P

CAP = 2
SRC, ROW, DEST, ENTRY, OWN, TABLE = 0, 64, 96, 128, 160, 256

VMEM = pl.BlockSpec(memory_space=pltpu.VMEM)
SMEM = pl.BlockSpec(memory_space=pltpu.SMEM)
ANY = pl.BlockSpec(memory_space=pl.ANY)
PARAMS = pltpu.CompilerParams(vmem_limit_bytes=32 << 20)


def dot(x, y, dims):
    return lax.dot_general(x, y, (dims, ((), ())), preferred_element_type=jnp.float32)


def shifted(block, by):
    count = lax.axis_size("tm")
    return lax.ppermute(block, "tm", [(i, (i + by) % count) for i in range(count)])


def exchanged(blocks):
    return lax.all_to_all(blocks, "basis", split_axis=0, concat_axis=0, tiled=True)


def plan_kernel(cols, me, wants, table, count):
    rows, per_row = cols.shape
    slots = wants.shape[0]
    for s in range(slots):
        wants[s] = -1
        table[ENTRY + s] = 0
    for o in range(slots // CAP):
        count[o] = 0
    for i in range(rows):
        for k in range(per_row):
            e = i * per_row + k
            col = cols[i, k]
            owner = col // rows
            row = col - owner * rows
            near = owner == me[0]

            @pl.when(near)
            def _():
                table[SRC + e] = row
                table[OWN + e] = row

            @pl.when(jnp.logical_not(near))
            def _():
                slot = owner * CAP + count[owner]
                count[owner] = count[owner] + 1
                wants[slot] = row
                table[SRC + e] = rows + slot
                table[OWN + e] = rows
                table[ENTRY + slot] = e


def merge_kernel(part, wanted, table):
    rows = 6
    for s in range(ROW, ROW + 32):
        w = wanted[s - ROW]
        table[s] = jnp.maximum(w, 0)
        table[s + DEST - ROW] = jnp.where(w < 0, rows, w)
    for s in list(range(ROW)) + list(range(ENTRY, TABLE)):
        table[s] = part[s]


def send_kernel(table, forward, adjoint, blocks, out, own, contrib, total, idx, sem):
    rows, per_row = blocks.shape[0], blocks.shape[1]
    copy = pltpu.make_async_copy(table, idx, sem)
    copy.start()
    for i in range(rows):
        x = adjoint[i]
        for k in range(per_row):
            contrib[i * per_row + k] = dot(x, blocks[i, k], ((1,), (0,)))
    total[...] = jnp.zeros_like(total)
    copy.wait()
    for o in range(out.shape[0]):
        for c in range(CAP):
            s = o * CAP + c
            out[o, c] = forward[idx[ROW + s]]
            out[o, CAP + c] = contrib[idx[ENTRY + s]].astype(out.dtype)
    for e in range(rows * per_row):
        total[idx[OWN + e]] += contrib[e]
    own[...] = total[:rows]


def receive_kernel(table, arrived, forward, own, blocks, store, image, adjoint, total, idx, sem):
    rows, per_row = blocks.shape[0], blocks.shape[1]
    copy = pltpu.make_async_copy(table, idx, sem)
    copy.start()
    store[:rows] = forward[...]
    for o in range(arrived.shape[0]):
        store[rows + CAP * o : rows + CAP * (o + 1)] = arrived[o, :CAP]
    total[:rows] = own[...]
    total[rows] = jnp.zeros_like(total[rows])
    copy.wait()
    for o in range(arrived.shape[0]):
        for c in range(CAP):
            total[idx[DEST + o * CAP + c]] += arrived[o, CAP + c].astype(jnp.float32)
    adjoint[...] = total[:rows].astype(adjoint.dtype)
    for i in range(rows):
        acc = None
        for k in range(per_row):
            term = dot(store[idx[SRC + i * per_row + k]], blocks[i, k], ((1,), (1,)))
            acc = term if acc is None else acc + term
        image[i] = acc.astype(image.dtype)


def pack_kernel(table, forward, out, idx, sem):
    copy = pltpu.make_async_copy(table, idx, sem)
    copy.start()
    copy.wait()
    for s in range(out.shape[0] * CAP):
        out[s // CAP, s % CAP] = forward[idx[ROW + s]]


def gradient_kernel(scale, turns, table, *refs):
    stores, adjoints = refs[: turns - 1], refs[turns - 1 : 2 * turns - 1]
    last, arrived, out, last_store, left, right, idx, sem = refs[2 * turns - 1 :]
    probes = left.shape[0] // turns
    rows = last.shape[0]
    per_row = out.shape[0] // rows
    width = out.shape[2]
    copy = pltpu.make_async_copy(table, idx, sem)
    copy.start()
    last_store[:rows] = last[...]
    for o in range(arrived.shape[0]):
        last_store[rows + CAP * o : rows + CAP * (o + 1)] = arrived[o]
    copy.wait()
    stores = (*stores, last_store)

    def row(i, carry):
        for h in range(turns):
            left[h * probes : (h + 1) * probes] = adjoints[turns - 1 - h][i]
        for k in range(per_row):
            source = idx[SRC + i * per_row + k]
            for h in range(turns):
                right[h * probes : (h + 1) * probes, k * width : (k + 1) * width] = stores[h][source]
        summed = dot(left[...], right[...], ((0,), (0,))) * scale
        for k in range(per_row):
            out[i * per_row + k] = summed[:, k * width : (k + 1) * width].astype(out.dtype)
        return carry

    lax.fori_loop(0, rows, row, 0)


def per_device(propagators, probes, block_cols):
    turns = lax.axis_size("tm")
    peers = lax.axis_size("basis")
    blocks = propagators[0]
    rows, per_row = block_cols.shape
    count, width = probes.shape[2:]
    slots = peers * CAP
    bf16, f32, i32 = jnp.bfloat16, jnp.float32, jnp.int32
    shape = jax.ShapeDtypeStruct
    index_scratch = [pltpu.SMEM((TABLE,), i32), pltpu.SemaphoreType.DMA(())]
    block_list = (rows, count, width)

    forward = probes[0]
    adjoint = shifted(forward, -1)
    wants, part = pl.pallas_call(
        plan_kernel,
        in_specs=[SMEM, SMEM],
        out_specs=[SMEM, SMEM],
        out_shape=[shape((slots,), i32), shape((TABLE,), i32)],
        scratch_shapes=[pltpu.SMEM((peers,), i32)],
    )(block_cols, lax.axis_index("basis").reshape(1))
    wanted = exchanged(wants.reshape(peers, CAP)).reshape(-1)
    table = pl.pallas_call(
        merge_kernel,
        in_specs=[SMEM, SMEM],
        out_specs=SMEM,
        out_shape=shape((TABLE,), i32),
    )(part, wanted)

    send = pl.pallas_call(
        send_kernel,
        in_specs=[ANY, VMEM, VMEM, VMEM],
        out_specs=[VMEM, VMEM],
        out_shape=[shape((peers, 2 * CAP, count, width), bf16), shape(block_list, f32)],
        scratch_shapes=[
            pltpu.VMEM((rows * per_row, count, width), f32),
            pltpu.VMEM((rows + 1, count, width), f32),
            *index_scratch,
        ],
        compiler_params=PARAMS,
    )
    receive = pl.pallas_call(
        receive_kernel,
        in_specs=[ANY, VMEM, VMEM, VMEM, VMEM],
        out_specs=[VMEM, VMEM, VMEM],
        out_shape=[shape((rows + slots, count, width), bf16), shape(block_list, bf16), shape(block_list, bf16)],
        scratch_shapes=[pltpu.VMEM((rows + 1, count, width), f32), *index_scratch],
        compiler_params=PARAMS,
    )
    stores, adjoints = [], [adjoint]
    for _ in range(turns - 1):
        outgoing, own = send(table, forward, adjoint, blocks)
        store, image, summed = receive(table, exchanged(outgoing), forward, own, blocks)
        forward, adjoint = shifted(image, 1), shifted(summed, -1)
        stores.append(store)
        adjoints.append(adjoint)
    last = pl.pallas_call(
        pack_kernel,
        in_specs=[ANY, VMEM],
        out_specs=VMEM,
        out_shape=shape((peers, CAP, count, width), bf16),
        scratch_shapes=index_scratch,
    )(table, forward)
    gradient = pl.pallas_call(
        functools.partial(gradient_kernel, 1.0 / math.sqrt(turns * count), turns),
        in_specs=[ANY] + [VMEM] * (2 * turns + 1),
        out_specs=VMEM,
        out_shape=shape((rows * per_row, width, width), bf16),
        scratch_shapes=[
            pltpu.VMEM((rows + slots, count, width), bf16),
            pltpu.VMEM((turns * count, width), bf16),
            pltpu.VMEM((turns * count, per_row * width), bf16),
            *index_scratch,
        ],
        compiler_params=PARAMS,
    )(table, *stores, *adjoints, forward, exchanged(last))
    return gradient.reshape(1, rows, per_row, width, width)


def solution(mesh):
    placed = (P("tm", "basis", None, None, None), P("tm", "basis", None, None), P("basis", None))
    return jax.shard_map(
        per_device,
        mesh=mesh,
        in_specs=placed,
        out_specs=P("tm", "basis", None, None, None),
        check_vma=False,
    )
```

```python
import functools
import math

import jax
import jax.numpy as jnp
from jax import lax
from jax.experimental import pallas as pl
from jax.experimental.pallas import tpu as pltpu
from jax.sharding import PartitionSpec as P

CAP = 2
SRC, ENTRY, OWN, TABLE = 0, 64, 128, 256

VMEM = pl.BlockSpec(memory_space=pltpu.VMEM)
SMEM = pl.BlockSpec(memory_space=pltpu.SMEM)
ANY = pl.BlockSpec(memory_space=pl.ANY)
SMALL = pltpu.CompilerParams(vmem_limit_bytes=4 << 20)
LARGE = pltpu.CompilerParams(vmem_limit_bytes=16 << 20)


def dot(x, y, dims=((1,), (0,))):
    return lax.dot_general(x, y, (dims, ((), ())), preferred_element_type=jnp.float32)


def shifted(block, by):
    count = lax.axis_size("tm")
    return lax.ppermute(block, "tm", [(i, (i + by) % count) for i in range(count)])


def exchanged(blocks):
    return lax.all_to_all(blocks, "basis", split_axis=0, concat_axis=0, tiled=True)


def plan_kernel(cols, me, wants, table, count, rows_of):
    rows, per_row = cols.shape
    peers = wants.shape[0]
    for s in range(peers * CAP):
        rows_of[s] = -1
        table[ENTRY + s] = 0
    for o in range(peers):
        count[o] = 0
    for i in range(rows):
        for k in range(per_row):
            e = i * per_row + k
            col = cols[i, k]
            owner = col // rows
            row = col - owner * rows
            near = owner == me[0]

            @pl.when(near)
            def _():
                table[SRC + e] = row
                table[OWN + e] = row

            @pl.when(jnp.logical_not(near))
            def _():
                slot = owner * CAP + count[owner]
                count[owner] = count[owner] + 1
                rows_of[slot] = row
                table[SRC + e] = rows + slot
                table[OWN + e] = rows
                table[ENTRY + slot] = e

    sublane = lax.broadcasted_iota(jnp.int32, wants.shape[1:], 0)
    for o in range(peers):
        wants[o] = jnp.where(sublane == 0, rows_of[CAP * o], rows_of[CAP * o + 1])


def select_kernel(wanted, pick, place):
    slots = wanted.shape[0] * CAP
    probes = pick.shape[0] // slots

    def at(shape, dim):
        index = lax.broadcasted_iota(jnp.int32, shape, dim)
        return index // probes, index % probes

    def ones(mask, like):
        return jnp.where(mask, 1.0, 0.0).astype(like.dtype)

    shape = (probes, pick.shape[1])
    row, probe = at(shape, 1)
    same = probe == at(shape, 0)[1]
    for s in range(slots):
        asked = jnp.broadcast_to(wanted[s // CAP][s % CAP : s % CAP + 1, : shape[1]], shape)
        pick[s * probes : (s + 1) * probes] = ones((asked == row) & same, pick)
    lanes = wanted.shape[2]
    shape = (place.shape[0], lanes)
    row, probe = at(shape, 0)
    slot, other = at(shape, 1)
    step = lanes // probes
    for g in range(slots // step):
        asked = jnp.full(shape, -1, jnp.int32)
        for j in range(step):
            s = g * step + j
            line = jnp.broadcast_to(wanted[s // CAP][s % CAP : s % CAP + 1, :], shape)
            asked = jnp.where(slot == j, line, asked)
        place[:, g * lanes : (g + 1) * lanes] = ones((asked == row) & (probe == other), place)


def turn_kernel(blocks, out):
    for i in range(blocks.shape[0]):
        for k in range(blocks.shape[1]):
            out[i, k] = blocks[i, k].T


def contribution_kernel(table, adjoint, blocks, out, own, contrib, total, idx, sem):
    rows, per_row = blocks.shape[:2]
    copy = pltpu.make_async_copy(table, idx, sem)
    copy.start()
    for i in range(rows):
        x = adjoint[i]
        for k in range(per_row):
            contrib[i * per_row + k] = dot(x, blocks[i, k])
    total[...] = jnp.zeros_like(total)
    copy.wait()
    for s in range(out.shape[0] * CAP):
        out[s // CAP, s % CAP] = contrib[idx[ENTRY + s]].astype(out.dtype)
    for e in range(rows * per_row):
        total[idx[OWN + e]] += contrib[e]
    own[...] = total[:rows]


def pack_kernel(pick, forward, contrib, out):
    rows, probes, width = forward.shape
    picked = dot(pick[...], forward[...].reshape(rows * probes, width)).astype(out.dtype)
    out[:, :CAP] = picked.reshape(out.shape[0], CAP, probes, width)
    if contrib is not None:
        out[:, CAP:] = contrib[...]


def sum_kernel(place, arrived, own, adjoint):
    rows, probes, width = own.shape
    blocks = arrived[:, CAP:].reshape(place.shape[1], width)
    total = own[...].reshape(rows * probes, width) + dot(place[...], blocks)
    adjoint[...] = total.astype(adjoint.dtype).reshape(rows, probes, width)


def image_kernel(table, arrived, forward, blocks, after, store, image, idx, sem):
    rows, per_row = blocks.shape[:2]
    copy = pltpu.make_async_copy(table, idx, sem)
    copy.start()
    store[:rows] = forward[...]
    for o in range(arrived.shape[0]):
        store[rows + CAP * o : rows + CAP * (o + 1)] = arrived[o, :CAP]
    copy.wait()
    for i in range(rows):
        acc = None
        for k in range(per_row):
            term = dot(store[idx[SRC + i * per_row + k]], blocks[i, k])
            acc = term if acc is None else acc + term
        image[i] = acc.astype(image.dtype)


def partial_kernel(turns, table, *refs):
    stores, adjoints = refs[:turns], refs[turns : 2 * turns]
    out, left, right, idx, sem, sems = refs[2 * turns :]
    probes = left.shape[1] // turns
    rows = left.shape[0]
    per_row = out.shape[0] // rows
    copies = [pltpu.make_async_copy(table, idx, sem)]
    for h in range(turns):
        part = pl.ds(h * probes, probes)
        copies.append(pltpu.make_async_copy(stores[h], right.at[:, part, :], sems.at[0, h]))
        copies.append(pltpu.make_async_copy(adjoints[h], left.at[:, part, :], sems.at[1, h]))
    for copy in copies:
        copy.start()
    for copy in copies:
        copy.wait()
    for i in range(rows):
        x = left[i].T
        for k in range(per_row):
            e = i * per_row + k
            out[e] = dot(x, right[idx[SRC + e]])


def gradient_kernel(scale, table, partial, arrived, forward, adjoint, out, store, right, idx, sem):
    rows, probes, width = forward.shape
    per_row = out.shape[0] // rows
    copy = pltpu.make_async_copy(table, idx, sem)
    copy.start()
    store[:rows] = forward[...]
    for o in range(arrived.shape[0]):
        store[rows + CAP * o : rows + CAP * (o + 1)] = arrived[o]
    copy.wait()
    for i in range(rows):
        for k in range(per_row):
            right[:, k * width : (k + 1) * width] = store[idx[SRC + i * per_row + k]]
        term = dot(adjoint[i], right[...], ((0,), (0,)))
        for k in range(per_row):
            e = i * per_row + k
            out[e] = ((partial[e] + term[:, k * width : (k + 1) * width]) * scale).astype(out.dtype)


def per_device(propagators, probes, block_cols):
    turns = lax.axis_size("tm")
    peers = lax.axis_size("basis")
    blocks = propagators[0]
    rows, per_row = block_cols.shape
    count, width = probes.shape[2:]
    slots = peers * CAP
    bf16, f32, i32 = jnp.bfloat16, jnp.float32, jnp.int32
    shape = jax.ShapeDtypeStruct
    index_scratch = [pltpu.SMEM((TABLE,), i32), pltpu.SemaphoreType.DMA(())]
    block_list = (rows, count, width)

    forward = probes[0]
    adjoint = shifted(forward, -1)
    wants, table = pl.pallas_call(
        plan_kernel,
        in_specs=[SMEM, SMEM],
        out_specs=[VMEM, SMEM],
        out_shape=[shape((peers, 8, width), i32), shape((TABLE,), i32)],
        scratch_shapes=[pltpu.SMEM((peers,), i32), pltpu.SMEM((slots,), i32)],
        compiler_params=SMALL,
        name="plan",
    )(block_cols, lax.axis_index("basis").reshape(1))
    pick, place = pl.pallas_call(
        select_kernel,
        in_specs=[VMEM],
        out_specs=[VMEM, VMEM],
        out_shape=[shape((slots * count, rows * count), bf16), shape((rows * count, slots * count), bf16)],
        compiler_params=SMALL,
        name="select",
    )(exchanged(wants))
    turned = pl.pallas_call(
        turn_kernel,
        in_specs=[VMEM],
        out_specs=VMEM,
        out_shape=shape(blocks.shape, bf16),
        compiler_params=SMALL,
        name="turned",
    )(blocks)

    contributions = pl.pallas_call(
        contribution_kernel,
        in_specs=[ANY, VMEM, VMEM],
        out_specs=[VMEM, VMEM],
        out_shape=[shape((peers, CAP, count, width), bf16), shape(block_list, f32)],
        scratch_shapes=[
            pltpu.VMEM((rows * per_row, count, width), f32),
            pltpu.VMEM((rows + 1, count, width), f32),
            *index_scratch,
        ],
        compiler_params=SMALL,
        name="contributions",
    )
    pack = pl.pallas_call(
        pack_kernel,
        in_specs=[VMEM, VMEM, VMEM],
        out_specs=VMEM,
        out_shape=shape((peers, 2 * CAP, count, width), bf16),
        compiler_params=SMALL,
        name="pack",
    )
    sums = pl.pallas_call(
        sum_kernel,
        in_specs=[VMEM, VMEM, VMEM],
        out_specs=VMEM,
        out_shape=shape(block_list, bf16),
        compiler_params=SMALL,
        name="sums",
    )
    images = pl.pallas_call(
        image_kernel,
        in_specs=[ANY, VMEM, VMEM, VMEM, ANY],
        out_specs=[VMEM, VMEM],
        out_shape=[shape((rows + slots, count, width), bf16), shape(block_list, bf16)],
        scratch_shapes=index_scratch,
        compiler_params=SMALL,
        name="images",
    )
    stores, adjoints = [], [adjoint]
    for _ in range(turns - 1):
        contrib, own = contributions(table, adjoint, blocks)
        arrived = exchanged(pack(pick, forward, contrib))
        summed = sums(place, arrived, own)
        adjoint = shifted(summed, -1)
        store, image = images(table, arrived, forward, turned, summed)
        forward = shifted(image, 1)
        stores.append(store)
        adjoints.append(adjoint)
    last = pl.pallas_call(
        lambda pick, forward, out: pack_kernel(pick, forward, None, out),
        in_specs=[VMEM, VMEM],
        out_specs=VMEM,
        out_shape=shape((peers, CAP, count, width), bf16),
        compiler_params=SMALL,
        name="pack_last",
    )(pick, forward)
    arrived = exchanged(last)
    partial = pl.pallas_call(
        functools.partial(partial_kernel, turns - 1),
        in_specs=[ANY] * (2 * turns - 1),
        out_specs=VMEM,
        out_shape=shape((rows * per_row, width, width), f32),
        scratch_shapes=[
            pltpu.VMEM((rows, (turns - 1) * count, width), bf16),
            pltpu.VMEM((rows + slots, (turns - 1) * count, width), bf16),
            *index_scratch,
            pltpu.SemaphoreType.DMA((2, turns - 1)),
        ],
        compiler_params=LARGE,
        name="partial",
    )(table, *stores, *adjoints[:0:-1])
    gradient = pl.pallas_call(
        functools.partial(gradient_kernel, 1.0 / math.sqrt(turns * count)),
        in_specs=[ANY] + [VMEM] * 4,
        out_specs=VMEM,
        out_shape=shape((rows * per_row, width, width), bf16),
        scratch_shapes=[
            pltpu.VMEM((rows + slots, count, width), bf16),
            pltpu.VMEM((count, per_row * width), bf16),
            *index_scratch,
        ],
        compiler_params=LARGE,
        name="gradient",
    )(table, partial, arrived, forward, adjoints[0])
    return gradient.reshape(1, rows, per_row, width, width)


def solution(mesh):
    placed = (P("tm", "basis", None, None, None), P("tm", "basis", None, None), P("basis", None))
    return jax.shard_map(
        per_device,
        mesh=mesh,
        in_specs=placed,
        out_specs=P("tm", "basis", None, None, None),
        check_vma=False,
    )
```

```python
import functools
import math

import jax
import jax.numpy as jnp
from jax import lax
from jax.experimental import pallas as pl
from jax.experimental.pallas import tpu as pltpu
from jax.sharding import PartitionSpec as P

CAP = 2
SRC, ENTRY, OWN, FIRST, TABLE = 0, 64, 128, 192, 256

VMEM = pl.BlockSpec(memory_space=pltpu.VMEM)
SMEM = pl.BlockSpec(memory_space=pltpu.SMEM)
ANY = pl.BlockSpec(memory_space=pl.ANY)
HBM = pl.BlockSpec(memory_space=pltpu.HBM)
SMALL = pltpu.CompilerParams(vmem_limit_bytes=4 << 20)
LARGE = pltpu.CompilerParams(vmem_limit_bytes=16 << 20)


def dot(x, y, dims=((1,), (0,))):
    return lax.dot_general(x, y, (dims, ((), ())), preferred_element_type=jnp.float32)


def shifted(block, by):
    count = lax.axis_size("tm")
    return lax.ppermute(block, "tm", [(i, (i + by) % count) for i in range(count)])


def exchanged(blocks):
    return lax.all_to_all(blocks, "basis", split_axis=0, concat_axis=0, tiled=True)


def plan_kernel(cols, me, wants, table, count, rows_of):
    rows, per_row = cols.shape
    peers = wants.shape[0]
    for s in range(peers * CAP):
        rows_of[s] = -1
        table[ENTRY + s] = 0
        table[FIRST + s] = 0
    for o in range(peers):
        count[o] = 0
    for i in range(rows):
        for k in range(per_row):
            e = i * per_row + k
            col = cols[i, k]
            owner = col // rows
            row = col - owner * rows
            near = owner == me[0]

            @pl.when(near)
            def _():
                table[SRC + e] = row
                table[OWN + e] = row

            @pl.when(jnp.logical_not(near))
            def _():
                slot = owner * CAP + count[owner]
                count[owner] = count[owner] + 1
                rows_of[slot] = row
                table[SRC + e] = rows + slot
                table[OWN + e] = rows
                table[ENTRY + slot] = e
                table[FIRST + slot] = owner * (rows + CAP + 1) + row

    part = lax.broadcasted_iota(jnp.int32, wants.shape[1:], 0) // (wants.shape[1] // CAP)
    for o in range(peers):
        asked = jnp.where(part == 0, rows_of[CAP * o], rows_of[CAP * o + 1])
        wants[o] = asked.astype(jnp.float32).astype(wants.dtype)


def first_pack_kernel(forward, contrib, wants, out):
    rows = forward.shape[0]
    for o in range(out.shape[0]):
        out[o, :rows] = forward[...]
    out[:, rows : rows + CAP] = contrib[...]
    out[:, rows + CAP] = wants[...]


def select_kernel(arrived, pick, place):
    slots = arrived.shape[0] * CAP
    last = arrived.shape[1] - 1
    probes, lanes = arrived.shape[2:]
    lines = []
    for o in range(arrived.shape[0]):
        tile = arrived[o, last].astype(jnp.float32).astype(jnp.int32)
        lines.extend(tile[c * (probes // CAP) : c * (probes // CAP) + 1] for c in range(CAP))

    def at(shape, dim):
        index = lax.broadcasted_iota(jnp.int32, shape, dim)
        return index // probes, index % probes

    def ones(mask, like):
        return jnp.where(mask, 1.0, 0.0).astype(like.dtype)

    shape = (probes, pick.shape[1])
    row, probe = at(shape, 1)
    same = probe == at(shape, 0)[1]
    for s in range(slots):
        asked = jnp.broadcast_to(lines[s][:, : shape[1]], shape)
        pick[s * probes : (s + 1) * probes] = ones((asked == row) & same, pick)
    shape = (place.shape[0], lanes)
    row, probe = at(shape, 0)
    slot, other = at(shape, 1)
    step = lanes // probes
    for g in range(slots // step):
        asked = jnp.full(shape, -1, jnp.int32)
        for j in range(step):
            asked = jnp.where(slot == j, jnp.broadcast_to(lines[g * step + j], shape), asked)
        place[:, g * lanes : (g + 1) * lanes] = ones((asked == row) & (probe == other), place)


def turn_kernel(blocks, out):
    for i in range(blocks.shape[0]):
        for k in range(blocks.shape[1]):
            out[i, k] = blocks[i, k].T


def contribution_kernel(table, adjoint, blocks, out, own, contrib, total, idx, sem):
    rows, per_row = blocks.shape[:2]
    copy = pltpu.make_async_copy(table, idx, sem)
    copy.start()
    for i in range(rows):
        x = adjoint[i]
        for k in range(per_row):
            contrib[i * per_row + k] = dot(x, blocks[i, k])
    total[...] = jnp.zeros_like(total)
    copy.wait()
    for s in range(out.shape[0] * CAP):
        out[s // CAP, s % CAP] = contrib[idx[ENTRY + s]].astype(out.dtype)
    for e in range(rows * per_row):
        total[idx[OWN + e]] += contrib[e]
    own[...] = total[:rows]


def pack_kernel(pick, forward, contrib, out):
    rows, probes, width = forward.shape
    picked = dot(pick[...], forward[...].reshape(rows * probes, width)).astype(out.dtype)
    out[:, :CAP] = picked.reshape(out.shape[0], CAP, probes, width)
    if contrib is not None:
        out[:, CAP:] = contrib[...]


def sum_kernel(begin, place, arrived, own, adjoint):
    rows, probes, width = own.shape
    blocks = arrived[:, begin : begin + CAP].reshape(place.shape[1], width)
    total = own[...].reshape(rows * probes, width) + dot(place[...], blocks)
    adjoint[...] = total.astype(adjoint.dtype).reshape(rows, probes, width)


def image_kernel(first, table, arrived, forward, blocks, after, store, image, idx, sem):
    rows, per_row = blocks.shape[:2]
    copy = pltpu.make_async_copy(table, idx, sem)
    copy.start()
    store[:rows] = forward[...]
    if first:
        copy.wait()
        for s in range(store.shape[0] - rows):
            store[rows + s] = arrived[idx[FIRST + s]]
    else:
        for o in range(arrived.shape[0]):
            store[rows + CAP * o : rows + CAP * (o + 1)] = arrived[o, :CAP]
        copy.wait()
    for i in range(rows):
        acc = None
        for k in range(per_row):
            term = dot(store[idx[SRC + i * per_row + k]], blocks[i, k])
            acc = term if acc is None else acc + term
        image[i] = acc.astype(image.dtype)


def partial_kernel(turns, table, *refs):
    stores, adjoints = refs[:turns], refs[turns : 2 * turns]
    out, left, right, idx, sem, sems = refs[2 * turns :]
    probes = left.shape[1] // turns
    rows = left.shape[0]
    per_row = out.shape[0] // rows
    copies = [pltpu.make_async_copy(table, idx, sem)]
    for h in range(turns):
        part = pl.ds(h * probes, probes)
        copies.append(pltpu.make_async_copy(stores[h], right.at[:, part, :], sems.at[0, h]))
        copies.append(pltpu.make_async_copy(adjoints[h], left.at[:, part, :], sems.at[1, h]))
    for copy in copies:
        copy.start()
    for copy in copies:
        copy.wait()
    for i in range(rows):
        x = left[i].T
        for k in range(per_row):
            e = i * per_row + k
            out[e] = dot(x, right[idx[SRC + e]])


def gradient_kernel(scale, table, partial, arrived, forward, adjoint, out, store, right, idx, sem):
    rows, probes, width = forward.shape
    per_row = out.shape[0] // rows
    copy = pltpu.make_async_copy(table, idx, sem)
    copy.start()
    store[:rows] = forward[...]
    for o in range(arrived.shape[0]):
        store[rows + CAP * o : rows + CAP * (o + 1)] = arrived[o]
    copy.wait()
    for i in range(rows):
        for k in range(per_row):
            right[:, k * width : (k + 1) * width] = store[idx[SRC + i * per_row + k]]
        term = dot(adjoint[i], right[...], ((0,), (0,)))
        for k in range(per_row):
            e = i * per_row + k
            out[e] = ((partial[e] + term[:, k * width : (k + 1) * width]) * scale).astype(out.dtype)


def per_device(propagators, probes, block_cols):
    turns = lax.axis_size("tm")
    peers = lax.axis_size("basis")
    blocks = propagators[0]
    rows, per_row = block_cols.shape
    count, width = probes.shape[2:]
    slots = peers * CAP
    bf16, f32, i32 = jnp.bfloat16, jnp.float32, jnp.int32
    shape = jax.ShapeDtypeStruct
    index_scratch = [pltpu.SMEM((TABLE,), i32), pltpu.SemaphoreType.DMA(())]
    block_list = (rows, count, width)

    forward = probes[0]
    adjoint = shifted(forward, -1)
    wants, table = pl.pallas_call(
        plan_kernel,
        in_specs=[SMEM, SMEM],
        out_specs=[VMEM, SMEM],
        out_shape=[shape((peers, count, width), bf16), shape((TABLE,), i32)],
        scratch_shapes=[pltpu.SMEM((peers,), i32), pltpu.SMEM((slots,), i32)],
        compiler_params=SMALL,
        name="plan",
    )(block_cols, lax.axis_index("basis").reshape(1))
    turned = pl.pallas_call(
        turn_kernel,
        in_specs=[VMEM],
        out_specs=VMEM,
        out_shape=shape(blocks.shape, bf16),
        compiler_params=SMALL,
        name="turned",
    )(blocks)

    contributions = pl.pallas_call(
        contribution_kernel,
        in_specs=[ANY, VMEM, VMEM],
        out_specs=[VMEM, VMEM],
        out_shape=[shape((peers, CAP, count, width), bf16), shape(block_list, f32)],
        scratch_shapes=[
            pltpu.VMEM((rows * per_row, count, width), f32),
            pltpu.VMEM((rows + 1, count, width), f32),
            *index_scratch,
        ],
        compiler_params=SMALL,
        name="contributions",
    )
    pack = pl.pallas_call(
        pack_kernel,
        in_specs=[VMEM, VMEM, VMEM],
        out_specs=VMEM,
        out_shape=shape((peers, 2 * CAP, count, width), bf16),
        compiler_params=SMALL,
        name="pack",
    )

    def sums(begin, *operands):
        return pl.pallas_call(
            functools.partial(sum_kernel, begin),
            in_specs=[VMEM, VMEM, VMEM],
            out_specs=VMEM,
            out_shape=shape(block_list, bf16),
            compiler_params=SMALL,
            name="sums",
        )(*operands)

    def images(first, *operands):
        return pl.pallas_call(
            functools.partial(image_kernel, first),
            in_specs=[ANY, VMEM, VMEM, VMEM, ANY],
            out_specs=[VMEM, VMEM],
            out_shape=[shape((rows + slots, count, width), bf16), shape(block_list, bf16)],
            scratch_shapes=index_scratch,
            compiler_params=SMALL,
            name="images",
        )(*operands)

    stores, adjoints = [], [adjoint]
    for turn in range(turns - 1):
        first = turn == 0
        contrib, own = contributions(table, adjoint, blocks)
        if first:
            outgoing = pl.pallas_call(
                first_pack_kernel,
                in_specs=[VMEM, VMEM, VMEM],
                out_specs=VMEM,
                out_shape=shape((peers, rows + CAP + 1, count, width), bf16),
                compiler_params=SMALL,
                name="first_pack",
            )(forward, contrib, wants)
            arrived = exchanged(outgoing)
            pick, place = pl.pallas_call(
                select_kernel,
                in_specs=[VMEM],
                out_specs=[VMEM, VMEM],
                out_shape=[shape((slots * count, rows * count), bf16), shape((rows * count, slots * count), bf16)],
                compiler_params=SMALL,
                name="select",
            )(arrived)
        else:
            arrived = exchanged(pack(pick, forward, contrib))
        summed = sums(rows if first else CAP, place, arrived, own)
        adjoint = shifted(summed, -1)
        if first:
            arrived = arrived.reshape(-1, count, width)
        store, image = images(first, table, arrived, forward, turned, summed)
        forward = shifted(image, 1)
        stores.append(store)
        adjoints.append(adjoint)
    last = pl.pallas_call(
        lambda pick, forward, out: pack_kernel(pick, forward, None, out),
        in_specs=[VMEM, VMEM],
        out_specs=VMEM,
        out_shape=shape((peers, CAP, count, width), bf16),
        compiler_params=SMALL,
        name="pack_last",
    )(pick, forward)
    arrived = exchanged(last)
    partial = pl.pallas_call(
        functools.partial(partial_kernel, turns - 1),
        in_specs=[ANY] + [HBM] * (2 * turns - 2),
        out_specs=VMEM,
        out_shape=shape((rows * per_row, width, width), f32),
        scratch_shapes=[
            pltpu.VMEM((rows, (turns - 1) * count, width), bf16),
            pltpu.VMEM((rows + slots, (turns - 1) * count, width), bf16),
            *index_scratch,
            pltpu.SemaphoreType.DMA((2, turns - 1)),
        ],
        compiler_params=LARGE,
        name="partial",
    )(table, *[pltpu.with_memory_space_constraint(x, pltpu.HBM) for x in (*stores, *adjoints[:0:-1])])
    gradient = pl.pallas_call(
        functools.partial(gradient_kernel, 1.0 / math.sqrt(turns * count)),
        in_specs=[ANY] + [VMEM] * 4,
        out_specs=VMEM,
        out_shape=shape((rows * per_row, width, width), bf16),
        scratch_shapes=[
            pltpu.VMEM((rows + slots, count, width), bf16),
            pltpu.VMEM((count, per_row * width), bf16),
            *index_scratch,
        ],
        compiler_params=LARGE,
        name="gradient",
    )(table, partial, arrived, forward, adjoints[0])
    return gradient.reshape(1, rows, per_row, width, width)


def solution(mesh):
    placed = (P("tm", "basis", None, None, None), P("tm", "basis", None, None), P("basis", None))
    return jax.shard_map(
        per_device,
        mesh=mesh,
        in_specs=placed,
        out_specs=P("tm", "basis", None, None, None),
        check_vma=False,
    )
```

```python
import functools
import math

import jax
import jax.numpy as jnp
from jax import lax
from jax.experimental import pallas as pl
from jax.experimental.pallas import tpu as pltpu
from jax.sharding import PartitionSpec as P

CAP = 2
SRC, ENTRY, OWN, FIRST, TABLE = 0, 64, 128, 192, 256

VMEM = pl.BlockSpec(memory_space=pltpu.VMEM)
SMEM = pl.BlockSpec(memory_space=pltpu.SMEM)
ANY = pl.BlockSpec(memory_space=pl.ANY)
HBM = pl.BlockSpec(memory_space=pltpu.HBM)
SMALL = pltpu.CompilerParams(vmem_limit_bytes=4 << 20)
LARGE = pltpu.CompilerParams(vmem_limit_bytes=16 << 20)


def dot(x, y, dims=((1,), (0,))):
    return lax.dot_general(x, y, (dims, ((), ())), preferred_element_type=jnp.float32)


def shifted(block, by):
    count = lax.axis_size("tm")
    return lax.ppermute(block, "tm", [(i, (i + by) % count) for i in range(count)])


def exchanged(blocks):
    return lax.all_to_all(blocks, "basis", split_axis=0, concat_axis=0, tiled=True)


def plan_kernel(cols, me, wants, table, count, rows_of):
    rows, per_row = cols.shape
    peers = wants.shape[0]
    for s in range(peers * CAP):
        rows_of[s] = -1
        table[ENTRY + s] = 0
        table[FIRST + s] = 0
    for o in range(peers):
        count[o] = 0
    for i in range(rows):
        for k in range(per_row):
            e = i * per_row + k
            col = cols[i, k]
            owner = col // rows
            row = col - owner * rows
            near = owner == me[0]

            @pl.when(near)
            def _():
                table[SRC + e] = row
                table[OWN + e] = row

            @pl.when(jnp.logical_not(near))
            def _():
                slot = owner * CAP + count[owner]
                count[owner] = count[owner] + 1
                rows_of[slot] = row
                table[SRC + e] = rows + slot
                table[OWN + e] = rows
                table[ENTRY + slot] = e
                table[FIRST + slot] = owner * (rows + CAP + 1) + row

    part = lax.broadcasted_iota(jnp.int32, wants.shape[1:], 0) // (wants.shape[1] // CAP)
    for o in range(peers):
        asked = jnp.where(part == 0, rows_of[CAP * o], rows_of[CAP * o + 1])
        wants[o] = asked.astype(jnp.float32).astype(wants.dtype)


def first_pack_kernel(forward, contrib, wants, out):
    rows = forward.shape[0]
    for o in range(out.shape[0]):
        out[o, :rows] = forward[...]
    out[:, rows : rows + CAP] = contrib[...]
    out[:, rows + CAP] = wants[...]


def select_kernel(arrived, pick, place):
    slots = arrived.shape[0] * CAP
    last = arrived.shape[1] - 1
    probes, lanes = arrived.shape[2:]
    lines = []
    for o in range(arrived.shape[0]):
        tile = arrived[o, last].astype(jnp.float32).astype(jnp.int32)
        lines.extend(tile[c * (probes // CAP) : c * (probes // CAP) + 1] for c in range(CAP))

    def at(shape, dim):
        index = lax.broadcasted_iota(jnp.int32, shape, dim)
        return index // probes, index % probes

    def ones(mask, like):
        return jnp.where(mask, 1.0, 0.0).astype(like.dtype)

    shape = (probes, pick.shape[1])
    row, probe = at(shape, 1)
    same = probe == at(shape, 0)[1]
    for s in range(slots):
        asked = jnp.broadcast_to(lines[s][:, : shape[1]], shape)
        pick[s * probes : (s + 1) * probes] = ones((asked == row) & same, pick)
    shape = (place.shape[0], lanes)
    row, probe = at(shape, 0)
    slot, other = at(shape, 1)
    step = lanes // probes
    for g in range(slots // step):
        asked = jnp.full(shape, -1, jnp.int32)
        for j in range(step):
            asked = jnp.where(slot == j, jnp.broadcast_to(lines[g * step + j], shape), asked)
        place[:, g * lanes : (g + 1) * lanes] = ones((asked == row) & (probe == other), place)


def turn_kernel(blocks, out):
    for i in range(blocks.shape[0]):
        for k in range(blocks.shape[1]):
            out[i, k] = blocks[i, k].T


def contribution_kernel(table, adjoint, blocks, out, own, contrib, total, idx, sem):
    rows, per_row = blocks.shape[:2]
    copy = pltpu.make_async_copy(table, idx, sem)
    copy.start()
    for i in range(rows):
        x = adjoint[i]
        for k in range(per_row):
            contrib[i * per_row + k] = dot(x, blocks[i, k])
    total[...] = jnp.zeros_like(total)
    copy.wait()
    for s in range(out.shape[0] * CAP):
        out[s // CAP, s % CAP] = contrib[idx[ENTRY + s]].astype(out.dtype)
    for e in range(rows * per_row):
        total[idx[OWN + e]] += contrib[e]
    own[...] = total[:rows]


def pack_kernel(pick, forward, contrib, out):
    rows, probes, width = forward.shape
    picked = dot(pick[...], forward[...].reshape(rows * probes, width)).astype(out.dtype)
    out[:, :CAP] = picked.reshape(out.shape[0], CAP, probes, width)
    if contrib is not None:
        out[:, CAP:] = contrib[...]


def turn_end_kernel(first, table, arrived, forward, blocks, place, own, store, image, adjoint, idx, sem):
    rows, per_row, width = blocks.shape[:3]
    probes = own.shape[1]
    begin = rows if first else CAP
    copy = pltpu.make_async_copy(table, idx, sem)
    copy.start()
    store[:rows] = forward[...]
    if not first:
        for o in range(arrived.shape[0]):
            store[rows + CAP * o : rows + CAP * (o + 1)] = arrived[o, :CAP]
    added = dot(place[...], arrived[:, begin : begin + CAP].reshape(place.shape[1], width))
    total = own[...].reshape(rows * probes, width) + added
    adjoint[...] = total.astype(adjoint.dtype).reshape(rows, probes, width)
    copy.wait()
    if first:
        for s in range(store.shape[0] - rows):
            o, block = idx[FIRST + s] // arrived.shape[1], idx[FIRST + s] % arrived.shape[1]
            store[rows + s] = arrived[o, block]
    for i in range(rows):
        sources = [store[idx[SRC + i * per_row + k]] for k in range(per_row)]
        term = dot(jnp.concatenate(sources, 1), blocks[i].reshape(per_row * width, width))
        image[i] = term.astype(image.dtype)


def partial_kernel(turns, table, *refs):
    stores, adjoints = refs[:turns], refs[turns : 2 * turns]
    out, left, right, idx, sem, sems = refs[2 * turns :]
    probes = left.shape[1] // turns
    rows = left.shape[0]
    per_row = out.shape[0] // rows
    copies = [pltpu.make_async_copy(table, idx, sem)]
    for h in range(turns):
        part = pl.ds(h * probes, probes)
        copies.append(pltpu.make_async_copy(stores[h], right.at[:, part, :], sems.at[0, h]))
        copies.append(pltpu.make_async_copy(adjoints[h], left.at[:, part, :], sems.at[1, h]))
    for copy in copies:
        copy.start()
    for copy in copies:
        copy.wait()
    for i in range(rows):
        x = left[i].T
        for k in range(per_row):
            e = i * per_row + k
            out[e] = dot(x, right[idx[SRC + e]])


def gradient_kernel(scale, table, partial, arrived, forward, adjoint, out, store, right, idx, sem):
    rows, probes, width = forward.shape
    per_row = out.shape[0] // rows
    copy = pltpu.make_async_copy(table, idx, sem)
    copy.start()
    store[:rows] = forward[...]
    for o in range(arrived.shape[0]):
        store[rows + CAP * o : rows + CAP * (o + 1)] = arrived[o]
    copy.wait()
    for i in range(rows):
        for k in range(per_row):
            right[:, k * width : (k + 1) * width] = store[idx[SRC + i * per_row + k]]
        term = dot(adjoint[i], right[...], ((0,), (0,)))
        for k in range(per_row):
            e = i * per_row + k
            out[e] = ((partial[e] + term[:, k * width : (k + 1) * width]) * scale).astype(out.dtype)


def per_device(propagators, probes, block_cols):
    turns = lax.axis_size("tm")
    peers = lax.axis_size("basis")
    blocks = propagators[0]
    rows, per_row = block_cols.shape
    count, width = probes.shape[2:]
    slots = peers * CAP
    bf16, f32, i32 = jnp.bfloat16, jnp.float32, jnp.int32
    shape = jax.ShapeDtypeStruct
    index_scratch = [pltpu.SMEM((TABLE,), i32), pltpu.SemaphoreType.DMA(())]
    block_list = (rows, count, width)

    forward = probes[0]
    adjoint = shifted(forward, -1)
    wants, table = pl.pallas_call(
        plan_kernel,
        in_specs=[SMEM, SMEM],
        out_specs=[VMEM, SMEM],
        out_shape=[shape((peers, count, width), bf16), shape((TABLE,), i32)],
        scratch_shapes=[pltpu.SMEM((peers,), i32), pltpu.SMEM((slots,), i32)],
        compiler_params=SMALL,
        name="plan",
    )(block_cols, lax.axis_index("basis").reshape(1))
    turned = pl.pallas_call(
        turn_kernel,
        in_specs=[VMEM],
        out_specs=VMEM,
        out_shape=shape(blocks.shape, bf16),
        compiler_params=SMALL,
        name="turned",
    )(blocks)

    contributions = pl.pallas_call(
        contribution_kernel,
        in_specs=[ANY, VMEM, VMEM],
        out_specs=[VMEM, VMEM],
        out_shape=[shape((peers, CAP, count, width), bf16), shape(block_list, f32)],
        scratch_shapes=[
            pltpu.VMEM((rows * per_row, count, width), f32),
            pltpu.VMEM((rows + 1, count, width), f32),
            *index_scratch,
        ],
        compiler_params=SMALL,
        name="contributions",
    )
    pack = pl.pallas_call(
        pack_kernel,
        in_specs=[VMEM, VMEM, VMEM],
        out_specs=VMEM,
        out_shape=shape((peers, 2 * CAP, count, width), bf16),
        compiler_params=SMALL,
        name="pack",
    )

    def turn_end(first, *operands):
        return pl.pallas_call(
            functools.partial(turn_end_kernel, first),
            in_specs=[ANY] + [VMEM] * 5,
            out_specs=[VMEM] * 3,
            out_shape=[shape((rows + slots, count, width), bf16), shape(block_list, bf16), shape(block_list, bf16)],
            scratch_shapes=index_scratch,
            compiler_params=SMALL,
            name="turn_end",
        )(*operands)

    stores, adjoints = [], [adjoint]
    for turn in range(turns - 1):
        first = turn == 0
        contrib, own = contributions(table, adjoint, blocks)
        if first:
            outgoing = pl.pallas_call(
                first_pack_kernel,
                in_specs=[VMEM, VMEM, VMEM],
                out_specs=VMEM,
                out_shape=shape((peers, rows + CAP + 1, count, width), bf16),
                compiler_params=SMALL,
                name="first_pack",
            )(forward, contrib, wants)
            arrived = exchanged(outgoing)
            pick, place = pl.pallas_call(
                select_kernel,
                in_specs=[VMEM],
                out_specs=[VMEM, VMEM],
                out_shape=[shape((slots * count, rows * count), bf16), shape((rows * count, slots * count), bf16)],
                compiler_params=SMALL,
                name="select",
            )(arrived)
        else:
            arrived = exchanged(pack(pick, forward, contrib))
        store, image, summed = turn_end(first, table, arrived, forward, turned, place, own)
        forward, adjoint = shifted(image, 1), shifted(summed, -1)
        stores.append(store)
        adjoints.append(adjoint)
    last = pl.pallas_call(
        lambda pick, forward, out: pack_kernel(pick, forward, None, out),
        in_specs=[VMEM, VMEM],
        out_specs=VMEM,
        out_shape=shape((peers, CAP, count, width), bf16),
        compiler_params=SMALL,
        name="pack_last",
    )(pick, forward)
    arrived = exchanged(last)
    partial = pl.pallas_call(
        functools.partial(partial_kernel, turns - 1),
        in_specs=[ANY] + [HBM] * (2 * turns - 2),
        out_specs=VMEM,
        out_shape=shape((rows * per_row, width, width), f32),
        scratch_shapes=[
            pltpu.VMEM((rows, (turns - 1) * count, width), bf16),
            pltpu.VMEM((rows + slots, (turns - 1) * count, width), bf16),
            *index_scratch,
            pltpu.SemaphoreType.DMA((2, turns - 1)),
        ],
        compiler_params=LARGE,
        name="partial",
    )(table, *[pltpu.with_memory_space_constraint(x, pltpu.HBM) for x in (*stores, *adjoints[:0:-1])])
    gradient = pl.pallas_call(
        functools.partial(gradient_kernel, 1.0 / math.sqrt(turns * count)),
        in_specs=[ANY] + [VMEM] * 4,
        out_specs=VMEM,
        out_shape=shape((rows * per_row, width, width), bf16),
        scratch_shapes=[
            pltpu.VMEM((rows + slots, count, width), bf16),
            pltpu.VMEM((count, per_row * width), bf16),
            *index_scratch,
        ],
        compiler_params=LARGE,
        name="gradient",
    )(table, partial, arrived, forward, adjoints[0])
    return gradient.reshape(1, rows, per_row, width, width)


def solution(mesh):
    placed = (P("tm", "basis", None, None, None), P("tm", "basis", None, None), P("basis", None))
    return jax.shard_map(
        per_device,
        mesh=mesh,
        in_specs=placed,
        out_specs=P("tm", "basis", None, None, None),
        check_vma=False,
    )
```

```python
import functools
import math

import jax
import jax.numpy as jnp
from jax import lax
from jax.experimental import pallas as pl
from jax.experimental.pallas import tpu as pltpu
from jax.sharding import PartitionSpec as P

CAP = 2
SRC, ENTRY, OWN, FIRST, TABLE = 0, 64, 128, 192, 256

VMEM = pl.BlockSpec(memory_space=pltpu.VMEM)
SMEM = pl.BlockSpec(memory_space=pltpu.SMEM)
ANY = pl.BlockSpec(memory_space=pl.ANY)
HBM = pl.BlockSpec(memory_space=pltpu.HBM)
SMALL = pltpu.CompilerParams(vmem_limit_bytes=4 << 20)
LARGE = pltpu.CompilerParams(vmem_limit_bytes=16 << 20)


def dot(x, y, dims=((1,), (0,))):
    return lax.dot_general(x, y, (dims, ((), ())), preferred_element_type=jnp.float32)


def shifted(block, by):
    count = lax.axis_size("tm")
    return lax.ppermute(block, "tm", [(i, (i + by) % count) for i in range(count)])


def exchanged(blocks):
    return lax.all_to_all(blocks, "basis", split_axis=0, concat_axis=0, tiled=True)


def plan_kernel(cols, me, wants, table, count, rows_of):
    rows, per_row = cols.shape
    peers = wants.shape[0]
    for s in range(peers * CAP):
        rows_of[s] = -1
        table[ENTRY + s] = 0
        table[FIRST + s] = 0
    for o in range(peers):
        count[o] = 0
    for i in range(rows):
        for k in range(per_row):
            e = i * per_row + k
            col = cols[i, k]
            owner = col // rows
            row = col - owner * rows
            near = owner == me[0]

            @pl.when(near)
            def _():
                table[SRC + e] = row
                table[OWN + e] = row

            @pl.when(jnp.logical_not(near))
            def _():
                slot = owner * CAP + count[owner]
                count[owner] = count[owner] + 1
                rows_of[slot] = row
                table[SRC + e] = rows + slot
                table[OWN + e] = rows
                table[ENTRY + slot] = e
                table[FIRST + slot] = owner * (rows + CAP + 1) + row

    part = lax.broadcasted_iota(jnp.int32, wants.shape[1:], 0) // (wants.shape[1] // CAP)
    for o in range(peers):
        asked = jnp.where(part == 0, rows_of[CAP * o], rows_of[CAP * o + 1])
        wants[o] = asked.astype(jnp.float32).astype(wants.dtype)


def first_pack_kernel(forward, contrib, wants, out):
    rows = forward.shape[0]
    for o in range(out.shape[0]):
        out[o, :rows] = forward[...]
    out[:, rows : rows + CAP] = contrib[...]
    out[:, rows + CAP] = wants[...]


def select_kernel(arrived, pick, place):
    slots = arrived.shape[0] * CAP
    last = arrived.shape[1] - 1
    probes, lanes = arrived.shape[2:]
    lines = []
    for o in range(arrived.shape[0]):
        tile = arrived[o, last].astype(jnp.float32).astype(jnp.int32)
        lines.extend(tile[c * (probes // CAP) : c * (probes // CAP) + 1] for c in range(CAP))

    def at(shape, dim):
        index = lax.broadcasted_iota(jnp.int32, shape, dim)
        return index // probes, index % probes

    def ones(mask, like):
        return jnp.where(mask, 1.0, 0.0).astype(like.dtype)

    shape = (probes, pick.shape[1])
    row, probe = at(shape, 1)
    same = probe == at(shape, 0)[1]
    for s in range(slots):
        asked = jnp.broadcast_to(lines[s][:, : shape[1]], shape)
        pick[s * probes : (s + 1) * probes] = ones((asked == row) & same, pick)
    shape = (place.shape[0], lanes)
    row, probe = at(shape, 0)
    slot, other = at(shape, 1)
    step = lanes // probes
    for g in range(slots // step):
        asked = jnp.full(shape, -1, jnp.int32)
        for j in range(step):
            asked = jnp.where(slot == j, jnp.broadcast_to(lines[g * step + j], shape), asked)
        place[:, g * lanes : (g + 1) * lanes] = ones((asked == row) & (probe == other), place)


def turn_kernel(blocks, out):
    for i in range(blocks.shape[0]):
        for k in range(blocks.shape[1]):
            out[i, k] = blocks[i, k].T


def contribution_kernel(table, adjoint, blocks, out, own, contrib, total, idx, sem):
    rows, per_row = blocks.shape[:2]
    copy = pltpu.make_async_copy(table, idx, sem)
    copy.start()
    for i in range(rows):
        joined = jnp.concatenate([blocks[i, k] for k in range(per_row)], 1)
        products = dot(adjoint[i], joined)
        width = blocks.shape[3]
        for k in range(per_row):
            contrib[i * per_row + k] = products[:, k * width : (k + 1) * width]
    total[...] = jnp.zeros_like(total)
    copy.wait()
    for s in range(out.shape[0] * CAP):
        out[s // CAP, s % CAP] = contrib[idx[ENTRY + s]].astype(out.dtype)
    for e in range(rows * per_row):
        total[idx[OWN + e]] += contrib[e]
    own[...] = total[:rows]


def pack_kernel(pick, forward, contrib, out):
    rows, probes, width = forward.shape
    picked = dot(pick[...], forward[...].reshape(rows * probes, width)).astype(out.dtype)
    out[:, :CAP] = picked.reshape(out.shape[0], CAP, probes, width)
    if contrib is not None:
        out[:, CAP:] = contrib[...]


def turn_end_kernel(first, table, arrived, forward, blocks, place, own, store, image, adjoint, idx, sem):
    rows, per_row, width = blocks.shape[:3]
    probes = own.shape[1]
    begin = rows if first else CAP
    copy = pltpu.make_async_copy(table, idx, sem)
    copy.start()
    store[:rows] = forward[...]
    if not first:
        for o in range(arrived.shape[0]):
            store[rows + CAP * o : rows + CAP * (o + 1)] = arrived[o, :CAP]
    added = dot(place[...], arrived[:, begin : begin + CAP].reshape(place.shape[1], width))
    total = own[...].reshape(rows * probes, width) + added
    adjoint[...] = total.astype(adjoint.dtype).reshape(rows, probes, width)
    copy.wait()
    if first:
        for s in range(store.shape[0] - rows):
            o, block = idx[FIRST + s] // arrived.shape[1], idx[FIRST + s] % arrived.shape[1]
            store[rows + s] = arrived[o, block]
    for i in range(rows):
        sources = [store[idx[SRC + i * per_row + k]] for k in range(per_row)]
        term = dot(jnp.concatenate(sources, 1), blocks[i].reshape(per_row * width, width))
        image[i] = term.astype(image.dtype)


def partial_kernel(turns, table, *refs):
    stores, adjoints = refs[:turns], refs[turns : 2 * turns]
    out, left, right, idx, sem, sems = refs[2 * turns :]
    probes = left.shape[1] // turns
    rows = left.shape[0]
    per_row = out.shape[0] // rows
    copies = [pltpu.make_async_copy(table, idx, sem)]
    for h in range(turns):
        part = pl.ds(h * probes, probes)
        copies.append(pltpu.make_async_copy(stores[h], right.at[:, part, :], sems.at[0, h]))
        copies.append(pltpu.make_async_copy(adjoints[h], left.at[:, part, :], sems.at[1, h]))
    for copy in copies:
        copy.start()
    for copy in copies:
        copy.wait()
    for i in range(rows):
        x = left[i].T
        for k in range(per_row):
            e = i * per_row + k
            out[e] = dot(x, right[idx[SRC + e]])


def gradient_kernel(scale, table, partial, arrived, forward, adjoint, out, store, right, idx, sem):
    rows, probes, width = forward.shape
    per_row = out.shape[0] // rows
    copy = pltpu.make_async_copy(table, idx, sem)
    copy.start()
    store[:rows] = forward[...]
    for o in range(arrived.shape[0]):
        store[rows + CAP * o : rows + CAP * (o + 1)] = arrived[o]
    copy.wait()
    for i in range(rows):
        for k in range(per_row):
            right[:, k * width : (k + 1) * width] = store[idx[SRC + i * per_row + k]]
        term = dot(adjoint[i], right[...], ((0,), (0,)))
        for k in range(per_row):
            e = i * per_row + k
            out[e] = ((partial[e] + term[:, k * width : (k + 1) * width]) * scale).astype(out.dtype)


def per_device(propagators, probes, block_cols):
    turns = lax.axis_size("tm")
    peers = lax.axis_size("basis")
    blocks = propagators[0]
    rows, per_row = block_cols.shape
    count, width = probes.shape[2:]
    slots = peers * CAP
    bf16, f32, i32 = jnp.bfloat16, jnp.float32, jnp.int32
    shape = jax.ShapeDtypeStruct
    index_scratch = [pltpu.SMEM((TABLE,), i32), pltpu.SemaphoreType.DMA(())]
    block_list = (rows, count, width)

    forward = probes[0]
    adjoint = shifted(forward, -1)
    wants, table = pl.pallas_call(
        plan_kernel,
        in_specs=[SMEM, SMEM],
        out_specs=[VMEM, SMEM],
        out_shape=[shape((peers, count, width), bf16), shape((TABLE,), i32)],
        scratch_shapes=[pltpu.SMEM((peers,), i32), pltpu.SMEM((slots,), i32)],
        compiler_params=SMALL,
        name="plan",
    )(block_cols, lax.axis_index("basis").reshape(1))
    turned = pl.pallas_call(
        turn_kernel,
        in_specs=[VMEM],
        out_specs=VMEM,
        out_shape=shape(blocks.shape, bf16),
        compiler_params=SMALL,
        name="turned",
    )(blocks)

    contributions = pl.pallas_call(
        contribution_kernel,
        in_specs=[ANY, VMEM, VMEM],
        out_specs=[VMEM, VMEM],
        out_shape=[shape((peers, CAP, count, width), bf16), shape(block_list, f32)],
        scratch_shapes=[
            pltpu.VMEM((rows * per_row, count, width), f32),
            pltpu.VMEM((rows + 1, count, width), f32),
            *index_scratch,
        ],
        compiler_params=SMALL,
        name="contributions",
    )
    pack = pl.pallas_call(
        pack_kernel,
        in_specs=[VMEM, VMEM, VMEM],
        out_specs=VMEM,
        out_shape=shape((peers, 2 * CAP, count, width), bf16),
        compiler_params=SMALL,
        name="pack",
    )

    def turn_end(first, *operands):
        return pl.pallas_call(
            functools.partial(turn_end_kernel, first),
            in_specs=[ANY] + [VMEM] * 5,
            out_specs=[VMEM] * 3,
            out_shape=[shape((rows + slots, count, width), bf16), shape(block_list, bf16), shape(block_list, bf16)],
            scratch_shapes=index_scratch,
            compiler_params=SMALL,
            name="turn_end",
        )(*operands)

    stores, adjoints = [], [adjoint]
    for turn in range(turns - 1):
        first = turn == 0
        contrib, own = contributions(table, adjoint, blocks)
        if first:
            outgoing = pl.pallas_call(
                first_pack_kernel,
                in_specs=[VMEM, VMEM, VMEM],
                out_specs=VMEM,
                out_shape=shape((peers, rows + CAP + 1, count, width), bf16),
                compiler_params=SMALL,
                name="first_pack",
            )(forward, contrib, wants)
            arrived = exchanged(outgoing)
            pick, place = pl.pallas_call(
                select_kernel,
                in_specs=[VMEM],
                out_specs=[VMEM, VMEM],
                out_shape=[shape((slots * count, rows * count), bf16), shape((rows * count, slots * count), bf16)],
                compiler_params=SMALL,
                name="select",
            )(arrived)
        else:
            arrived = exchanged(pack(pick, forward, contrib))
        store, image, summed = turn_end(first, table, arrived, forward, turned, place, own)
        forward, adjoint = shifted(image, 1), shifted(summed, -1)
        stores.append(store)
        adjoints.append(adjoint)
    last = pl.pallas_call(
        lambda pick, forward, out: pack_kernel(pick, forward, None, out),
        in_specs=[VMEM, VMEM],
        out_specs=VMEM,
        out_shape=shape((peers, CAP, count, width), bf16),
        compiler_params=SMALL,
        name="pack_last",
    )(pick, forward)
    arrived = exchanged(last)
    partial = pl.pallas_call(
        functools.partial(partial_kernel, turns - 1),
        in_specs=[ANY] + [HBM] * (2 * turns - 2),
        out_specs=VMEM,
        out_shape=shape((rows * per_row, width, width), f32),
        scratch_shapes=[
            pltpu.VMEM((rows, (turns - 1) * count, width), bf16),
            pltpu.VMEM((rows + slots, (turns - 1) * count, width), bf16),
            *index_scratch,
            pltpu.SemaphoreType.DMA((2, turns - 1)),
        ],
        compiler_params=LARGE,
        name="partial",
    )(table, *[pltpu.with_memory_space_constraint(x, pltpu.HBM) for x in (*stores, *adjoints[:0:-1])])
    gradient = pl.pallas_call(
        functools.partial(gradient_kernel, 1.0 / math.sqrt(turns * count)),
        in_specs=[ANY] + [VMEM] * 4,
        out_specs=VMEM,
        out_shape=shape((rows * per_row, width, width), bf16),
        scratch_shapes=[
            pltpu.VMEM((rows + slots, count, width), bf16),
            pltpu.VMEM((count, per_row * width), bf16),
            *index_scratch,
        ],
        compiler_params=LARGE,
        name="gradient",
    )(table, partial, arrived, forward, adjoints[0])
    return gradient.reshape(1, rows, per_row, width, width)


def solution(mesh):
    placed = (P("tm", "basis", None, None, None), P("tm", "basis", None, None), P("basis", None))
    return jax.shard_map(
        per_device,
        mesh=mesh,
        in_specs=placed,
        out_specs=P("tm", "basis", None, None, None),
        check_vma=False,
    )
```
